512 devices in a mesh: layer: 32 (over x_lo, y, core), tp: 16 (over z, x_hi).
Axes of the slice: x: 4 (x_hi: 2, x_lo: 2; x = x_hi * 2 + x_lo), y: 8, z: 8, core: 2. Of those that a mesh axis runs over, the one named last changes fastest.
Arguments:
- acts: bfloat16 [4096, 2048], P(('layer', 'tp')), may hold values from -12 to 12, as said below
- fresh: bfloat16 [2, 128, 2048], P(None, 'tp'), may hold values from -12 to 12, as said below
- norm_first: float32 [16, 2048], replicated, may hold values from 0.5 to 1.5
- norm_second: float32 [16, 2048], replicated, may hold values from 0.5 to 1.5
- proj_qkv: bfloat16 [512, 2048, 192], P(('layer', 'tp')), may hold values from -1 to 1
- proj_out: bfloat16 [32768, 2048], P(('layer', 'tp')), may hold values from -0.125 to 0.125
- proj_gate_up: bfloat16 [2048, 2, 131072], P(None, None, ('layer', 'tp')), may hold values from -0.125 to 0.125
- proj_down: bfloat16 [131072, 2048], P(('layer', 'tp')), may hold values from -0.0625 to 0.0625
- memory_state: float32 [512, 64, 64], P(('layer', 'tp')), may hold values from -768 to 768
- memory_norm: float32 [512, 64], P(('layer', 'tp')), may hold values from 16 to 256
- bias_gate: float32 [512], P(('layer', 'tp')), may hold values from -3 to 3
Outputs:
- first_out: bfloat16 [4096, 2048], P(('layer', 'tp'))
- second_out: bfloat16 [4096, 2048], P(('layer', 'tp'))
- memory_after: float32 [512, 64, 64], P(('layer', 'tp'))
- norm_after: float32 [512, 64], P(('layer', 'tp'))
The draws below stay inside these ranges and needn't reach their ends.
Inputs may be any that keep to these rules, and one draw needn't show every extreme that they name: `acts`: activation rows. `fresh`: activation rows.
All inputs are finite; a program needn't handle non-finite values.
Results may differ from the reference program's by a relative error of at most 0.025.
Values may be sent and summed in bfloat16 or wider, within the bound.
No kernel may reach another device: no remote copies, remote signals or barrier semaphores. Data moves between devices by JAX's collectives and lax.ppermute only.
A program may use at most 64 MiB of HBM per device.

```python
import math
import jax
import jax.numpy as jnp
from jax import lax

D = 2048
DH = 64
HEADS_DEV = 1
FF_DEV = 256
SEG = 256
HEADS = 32
FF = 8192
LAYERS = 16


def stream_draw(key, leading):
    base_key = jax.random.fold_in(key, 0)
    values = jax.random.normal(base_key, leading + (D,), jnp.float32)
    return jnp.clip(values, -12.0, 12.0)


def draw_acts(key, part):
    return stream_draw(key, (LAYERS * SEG,)).astype(jnp.bfloat16)


def draw_fresh(key, part):
    return stream_draw(key, (2, SEG // 2)).astype(jnp.bfloat16)


def draw_proj_qkv(key, part):
    key_one = jax.random.fold_in(key, 0)
    values = jax.random.normal(key_one, (LAYERS * HEADS, D, 3 * DH), jnp.float32) * D ** (-0.5)
    return jnp.clip(values, -1.0, 1.0).astype(jnp.bfloat16)


def shard_levels(rng, shape, cuts, smallest, top_value):
    gain = 1.0
    for axis_at, blocks in cuts:
        steps = jax.random.uniform(jax.random.fold_in(jax.random.fold_in(rng, 6), axis_at), (blocks,), jnp.float32, smallest / len(cuts), top_value / len(cuts))
        gain = gain * jnp.repeat(jnp.exp(steps), shape[axis_at] // blocks).reshape((-1,) + (1,) * (len(shape) - 1 - axis_at))
    return gain


def centred(own_key, extent, deviation, reach, cuts=(), dtype=jnp.bfloat16):
    values = jax.random.normal(own_key, extent, jnp.float32) * deviation
    if len(cuts) > 0:
        values = shard_levels(own_key, extent, cuts, -0.22, 0.18) * values
    return jnp.clip(values, min=-reach, max=reach).astype(dtype)


def setup_inputs(seed: int = 0) -> dict:
    key_of = jax.random.split(jax.random.key(seed), 12)
    acts = draw_acts(jax.random.fold_in(key_of[11], 71), 0)
    fresh = draw_fresh(jax.random.fold_in(key_of[11], 71), 0)
    norm_first = jnp.clip(1.0 + 0.1 * jax.random.normal(key_of[2], (LAYERS, D), jnp.float32), 0.5, 1.5)
    norm_second = jnp.clip(1.0 + 0.1 * jax.random.normal(key_of[3], (LAYERS, D), jnp.float32), 0.5, 1.5)
    proj_qkv = draw_proj_qkv(jax.random.fold_in(key_of[11], 71), 0)
    proj_out = centred(key_of[5], (LAYERS * HEADS * DH, D), (HEADS * DH) ** -0.5, 0.125, ((0, 512),))
    proj_gate_up = centred(key_of[6], (D, 2, LAYERS * FF), D ** -0.5, 0.125, ((2, 512),))
    proj_down = centred(key_of[7], (LAYERS * FF, D), FF ** -0.5, 0.0625, ((0, 512),))
    memory_state = centred(key_of[8], (LAYERS * HEADS, DH, DH), 128.0, 768.0, ((0, 512),), jnp.float32)
    memory_norm = jnp.clip(jnp.exp(math.log(256.0) - 2.7725887 * jax.random.uniform(key_of[9], (LAYERS * HEADS, DH), jnp.float32) ** shard_levels(key_of[9], (LAYERS * HEADS, DH), ((0, 512),), -0.2, 0.2)), 16.0, 256.0)
    bias_gate = jnp.clip(jax.random.uniform(key_of[10], (LAYERS * HEADS,), jnp.float32, -3.0, 3.0) * shard_levels(key_of[10], (LAYERS * HEADS,), ((0, 512),), -0.4, 0.0), -3.0, 3.0)
    return {"acts": acts, "fresh": fresh, "norm_first": norm_first, "norm_second": norm_second, "proj_qkv": proj_qkv, "proj_out": proj_out, "proj_gate_up": proj_gate_up, "proj_down": proj_down, "memory_state": memory_state, "memory_norm": memory_norm, "bias_gate": bias_gate}


def rms_norm(values, weight):
    floats = values.astype(jnp.float32)
    scaled = floats * lax.rsqrt(lax.optimization_barrier(jnp.mean(floats * floats, axis=-1, keepdims=True)) + 1e-05)
    return (scaled * weight).astype(jnp.bfloat16)

def one_layer(stream, gain_one, gain_two, weight_qkv, weight_out, weight_gu, weight_down, memory, totals, logits):
    head_dim = memory.shape[-1]
    seg_len = stream.shape[0]
    width = weight_out.shape[1]
    normed = rms_norm(stream, gain_one)
    qkv = jnp.einsum('sd,hdc->shc', normed.astype(jnp.float32), weight_qkv.astype(jnp.float32)).astype(jnp.bfloat16)
    queries = qkv[..., :head_dim].astype(jnp.float32)
    keyed = qkv[..., head_dim:2 * head_dim].astype(jnp.float32)
    valued = qkv[..., 2 * head_dim:].astype(jnp.float32)
    scores = jnp.einsum('qhc,khc->hqk', queries, keyed) * head_dim ** (-0.5)
    positions = jnp.arange(seg_len)
    allowed = positions[:, None] >= positions[None, :]
    probs = jax.nn.softmax(jnp.where(allowed[None], scores, -jnp.inf), axis=-1).astype(jnp.bfloat16)
    direct = jnp.einsum('hqk,khc->qhc', probs.astype(jnp.float32), valued)
    lifted_q = jax.nn.elu(queries) + 1.0
    lifted_k = jax.nn.elu(keyed) + 1.0
    numer = jnp.einsum('qhc,hce->qhe', lifted_q, memory, precision=lax.Precision.HIGHEST)
    denom = jnp.einsum('qhc,hc->qh', lifted_q, totals, precision=lax.Precision.HIGHEST)[..., None]
    gate_open = jax.nn.sigmoid(logits)[None, :, None]
    blended = (gate_open * numer / denom + (1.0 - gate_open) * direct).astype(jnp.bfloat16)
    new_memory = memory + jnp.einsum('khc,khe->hce', lifted_k, valued, precision=lax.Precision.HIGHEST)
    new_totals = totals + lax.optimization_barrier(jnp.sum(lifted_k, axis=0))
    head_groups = HEADS // HEADS_DEV
    grouped = blended.reshape(seg_len, head_groups, -1).astype(jnp.float32)
    parts = jnp.einsum('snk,nkd->nsd', grouped, weight_out.reshape(head_groups, -1, width).astype(jnp.float32))
    rounded = lax.optimization_barrier(parts.astype(jnp.bfloat16))
    attn = lax.optimization_barrier(jnp.sum(rounded.astype(jnp.float32), axis=0))
    hidden_one = (stream.astype(jnp.float32) + attn).astype(jnp.bfloat16)
    normed_two = rms_norm(hidden_one, gain_two)
    gate_up = jnp.einsum('sd,dtf->stf', normed_two.astype(jnp.float32), weight_gu.astype(jnp.float32))
    hidden = (jax.nn.silu(gate_up[:, 0]) * gate_up[:, 1]).astype(jnp.bfloat16)
    unit_groups = FF // FF_DEV
    dparts = jnp.einsum('snf,nfd->nsd', hidden.reshape(seg_len, unit_groups, -1).astype(jnp.float32), weight_down.reshape(unit_groups, -1, width).astype(jnp.float32))
    drounded = lax.optimization_barrier(dparts.astype(jnp.bfloat16))
    ffn = lax.optimization_barrier(jnp.sum(drounded.astype(jnp.float32), axis=0))
    output = (hidden_one.astype(jnp.float32) + ffn).astype(jnp.bfloat16)
    return (output, new_memory, new_totals)

def reference(acts, fresh, norm_first, norm_second, proj_qkv, proj_out, proj_gate_up, proj_down, memory_state, memory_norm, bias_gate):
    acts_l = acts.reshape(LAYERS, SEG, D)
    fresh_rows = fresh.reshape(SEG, D)
    qkv_l = proj_qkv.reshape(LAYERS, HEADS, D, 3 * DH)
    out_l = proj_out.reshape(LAYERS, HEADS * DH, D)
    gu_l = jnp.transpose(proj_gate_up.reshape(D, 2, LAYERS, FF), (2, 0, 1, 3))
    down_l = proj_down.reshape(LAYERS, FF, D)
    memory_l = memory_state.reshape(LAYERS, HEADS, DH, DH)
    totals_l = memory_norm.reshape(LAYERS, HEADS, DH)
    bias_l = bias_gate.reshape(LAYERS, HEADS)

    def run_all(inputs, memory, totals):
        return lax.map(lambda items: one_layer(*items), (inputs, norm_first, norm_second, qkv_l, out_l, gu_l, down_l, memory, totals, bias_l))
    first_out, memory_one, totals_one = run_all(acts_l, memory_l, totals_l)
    incoming = jnp.concatenate([fresh_rows[None], first_out[:-1]], axis=0)
    second_out, memory_two, totals_two = run_all(incoming, memory_one, totals_one)
    return (first_out.reshape(LAYERS * SEG, D), second_out.reshape(LAYERS * SEG, D), memory_two.reshape(LAYERS * HEADS, DH, DH), totals_two.reshape(LAYERS * HEADS, DH))
```

```python
import jax
import jax.numpy as jnp
from jax import lax
from jax.sharding import PartitionSpec as P


def swap_halves(value):
    pairs = [(source, source ^ 1) for source in range(lax.axis_size("layer"))]
    return lax.ppermute(value, "layer", pairs)


def next_layer(value):
    count = lax.axis_size("layer")
    return lax.ppermute(value, "layer", [(source, source + 2) for source in range(count - 2)])


def exchange(blocks):
    return lax.all_to_all(blocks, "tp", 0, 0, tiled=True)


def gather_rows(rows):
    members = lax.axis_size("tp")
    blocks = exchange(jnp.broadcast_to(rows[None], (members,) + rows.shape))
    return blocks.reshape((-1, rows.shape[1]))


def scatter_sum(partial):
    members = lax.axis_size("tp")
    blocks = exchange(partial.reshape((members, -1, partial.shape[1])))
    return jnp.sum(blocks.astype(jnp.float32), axis=0)


def rms_norm(values, weight):
    floats = values.astype(jnp.float32)
    scaled = floats * lax.rsqrt(jnp.mean(floats * floats, axis=-1, keepdims=True) + 1e-05)
    return (scaled * weight).astype(jnp.bfloat16)


def attend(qkv, memory, totals, logits, allowed):
    head_dim = memory.shape[-1]
    queries = qkv[..., :head_dim]
    keyed = qkv[..., head_dim : 2 * head_dim]
    valued = qkv[..., 2 * head_dim :]
    scores = jnp.einsum(
        "qhc,khc->hqk", queries, keyed, preferred_element_type=jnp.float32
    ) * head_dim ** (-0.5)
    probs = jax.nn.softmax(jnp.where(allowed[None], scores, -jnp.inf), axis=-1).astype(jnp.bfloat16)
    direct = jnp.einsum("hqk,khc->qhc", probs, valued, preferred_element_type=jnp.float32)
    lifted_q = jax.nn.elu(queries.astype(jnp.float32)) + 1.0
    lifted_k = jax.nn.elu(keyed.astype(jnp.float32)) + 1.0
    numer = jnp.einsum("qhc,hce->qhe", lifted_q, memory, precision=lax.Precision.HIGHEST)
    denom = jnp.einsum("qhc,hc->qh", lifted_q, totals, precision=lax.Precision.HIGHEST)[..., None]
    gate_open = jax.nn.sigmoid(logits)[None, :, None]
    blended = (gate_open * numer / denom + (1.0 - gate_open) * direct).astype(jnp.bfloat16)
    new_memory = memory + jnp.einsum(
        "khc,khe->hce", lifted_k, valued.astype(jnp.float32), precision=lax.Precision.HIGHEST
    )
    new_totals = totals + jnp.sum(lifted_k, axis=0)
    return (blended.reshape(qkv.shape[0], -1), new_memory, new_totals)


def body(
    acts,
    fresh,
    norm_first,
    norm_second,
    proj_qkv,
    proj_out,
    proj_gate_up,
    proj_down,
    memory_state,
    memory_norm,
    bias_gate,
):
    position = lax.axis_index("layer")
    half = position % 2
    depth = position // 2
    gain_one = lax.dynamic_index_in_dim(norm_first, depth, 0, keepdims=False)
    gain_two = lax.dynamic_index_in_dim(norm_second, depth, 0, keepdims=False)
    other_gate_up = swap_halves(proj_gate_up)
    other_down = swap_halves(proj_down)
    half_len = acts.shape[0] * lax.axis_size("tp")
    index = jnp.arange(2 * half_len)
    places = jnp.where(index < half_len, index + half * half_len, index - half * half_len)
    allowed = places[:, None] >= places[None, :]

    def project(rows):
        return jnp.einsum("sd,hdc->shc", rows, proj_qkv, preferred_element_type=jnp.float32).astype(
            jnp.bfloat16
        )

    def expand(rows, weight):
        gate_up = jnp.einsum("sd,dtf->stf", rows, weight, preferred_element_type=jnp.float32)
        return (jax.nn.silu(gate_up[:, 0]) * gate_up[:, 1]).astype(jnp.bfloat16)

    def apply_layer(rows, memory, totals):
        mine = gather_rows(rms_norm(rows, gain_one))
        normed = jnp.concatenate([mine, swap_halves(mine)], axis=0)
        blended, memory, totals = attend(project(normed), memory, totals, bias_gate, allowed)
        partial = jnp.dot(blended, proj_out, preferred_element_type=jnp.float32)
        away = swap_halves(partial[half_len:].astype(jnp.bfloat16))
        pair = (partial[:half_len] + away.astype(jnp.float32)).astype(jnp.bfloat16)
        hidden_one = (rows.astype(jnp.float32) + scatter_sum(pair)).astype(jnp.bfloat16)
        normed_two = gather_rows(rms_norm(hidden_one, gain_two))
        down = jnp.dot(
            expand(normed_two, proj_gate_up), proj_down, preferred_element_type=jnp.float32
        ) + jnp.dot(
            expand(normed_two, other_gate_up), other_down, preferred_element_type=jnp.float32
        )
        ffn = scatter_sum(down.astype(jnp.bfloat16))
        output = (hidden_one.astype(jnp.float32) + ffn).astype(jnp.bfloat16)
        return (output, memory, totals)

    first_rows, memory_one, totals_one = apply_layer(acts, memory_state, memory_norm)
    incoming = next_layer(first_rows)
    fresh_rows = lax.dynamic_index_in_dim(fresh, half, 0, keepdims=False)
    entering = jnp.where(depth == 0, fresh_rows, incoming)
    second_rows, memory_two, totals_two = apply_layer(entering, memory_one, totals_one)
    return (first_rows, second_rows, memory_two, totals_two)


def solution(mesh):
    in_specs = (
        P(("layer", "tp"), None),
        P(None, "tp", None),
        P(),
        P(),
        P(("layer", "tp"), None, None),
        P(("layer", "tp"), None),
        P(None, None, ("layer", "tp")),
        P(("layer", "tp"), None),
        P(("layer", "tp"), None, None),
        P(("layer", "tp"), None),
        P(("layer", "tp")),
    )
    out_specs = (
        P(("layer", "tp"), None),
        P(("layer", "tp"), None),
        P(("layer", "tp"), None, None),
        P(("layer", "tp"), None),
    )
    return jax.shard_map(body, mesh=mesh, in_specs=in_specs, out_specs=out_specs, check_vma=False)
```

```python
import jax
import jax.numpy as jnp
from jax import lax
from jax.sharding import PartitionSpec as P


def swap_halves(value):
    pairs = [(source, source ^ 1) for source in range(lax.axis_size("layer"))]
    return lax.ppermute(value, "layer", pairs)


def next_layer(value):
    count = lax.axis_size("layer")
    return lax.ppermute(value, "layer", [(source, source + 2) for source in range(count - 2)])


def exchange(blocks):
    return lax.all_to_all(blocks, "tp", 0, 0, tiled=True)


def gather_rows(rows):
    members = lax.axis_size("tp")
    blocks = exchange(jnp.broadcast_to(rows[None], (members,) + rows.shape))
    return blocks.reshape((-1, rows.shape[1]))


def scatter_sum(partial):
    members = lax.axis_size("tp")
    blocks = exchange(partial.reshape((members, -1, partial.shape[1])))
    return jnp.sum(blocks.astype(jnp.float32), axis=0)


def rms_norm(values, weight):
    floats = values.astype(jnp.float32)
    scaled = floats * lax.rsqrt(jnp.mean(floats * floats, axis=-1, keepdims=True) + 1e-05)
    return (scaled * weight).astype(jnp.bfloat16)


def lifted(values):
    return jax.nn.elu(values.astype(jnp.float32)) + 1.0


def attend(queries, keyed, valued, memory, totals, logits, allowed):
    head_dim = memory.shape[-1]
    scores = jnp.einsum(
        "qhc,khc->hqk", queries, keyed, preferred_element_type=jnp.float32
    ) * head_dim ** (-0.5)
    probs = jax.nn.softmax(jnp.where(allowed[None], scores, -jnp.inf), axis=-1).astype(jnp.bfloat16)
    direct = jnp.einsum("hqk,khc->qhc", probs, valued, preferred_element_type=jnp.float32)
    lifted_q = lifted(queries)
    numer = jnp.einsum("qhc,hce->qhe", lifted_q, memory, precision=lax.Precision.HIGHEST)
    denom = jnp.einsum("qhc,hc->qh", lifted_q, totals, precision=lax.Precision.HIGHEST)[..., None]
    gate_open = jax.nn.sigmoid(logits)[None, :, None]
    return (gate_open * numer / denom + (1.0 - gate_open) * direct).astype(jnp.bfloat16)


def absorb(keyed, valued, memory, totals):
    lifted_k = lifted(keyed)
    new_memory = memory + jnp.einsum(
        "khc,khe->hce", lifted_k, valued.astype(jnp.float32), precision=lax.Precision.HIGHEST
    )
    return (new_memory, totals + jnp.sum(lifted_k, axis=0))


def body(
    acts,
    fresh,
    norm_first,
    norm_second,
    proj_qkv,
    proj_out,
    proj_gate_up,
    proj_down,
    memory_state,
    memory_norm,
    bias_gate,
):
    position = lax.axis_index("layer")
    half = position % 2
    depth = position // 2
    gain_one = lax.dynamic_index_in_dim(norm_first, depth, 0, keepdims=False)
    gain_two = lax.dynamic_index_in_dim(norm_second, depth, 0, keepdims=False)
    head_dim = memory_state.shape[-1]
    half_len = acts.shape[0] * lax.axis_size("tp")
    logit_row = jnp.broadcast_to(bias_gate[:, None, None], (1, 1, head_dim))
    state = jnp.concatenate([memory_state, memory_norm[:, None], logit_row], axis=1)
    other_state = swap_halves(state)
    wide = lax.optimization_barrier(jnp.transpose(proj_gate_up, (1, 0, 2)))
    qkv_pair, out_pair, wide_pair, down_pair = (
        lax.optimization_barrier(jnp.concatenate([weight, swap_halves(weight)], axis=axis))
        for weight, axis in ((proj_qkv, 0), (proj_out, 0), (wide, 2), (proj_down, 0))
    )
    memory_pair = jnp.concatenate([memory_state, other_state[:, :head_dim]], axis=0)
    totals_pair = jnp.concatenate([memory_norm, other_state[:, head_dim]], axis=0)
    logits = jnp.concatenate([bias_gate, other_state[:, head_dim + 1, 0]], axis=0)
    index = jnp.arange(half_len)
    causal = index[:, None] >= index[None, :]
    allowed = jnp.concatenate([causal, jnp.broadcast_to(half == 1, causal.shape)], axis=1)

    def expand(rows):
        gate, up = (
            jnp.dot(rows, weight, preferred_element_type=jnp.float32) for weight in wide_pair
        )
        return (jax.nn.silu(gate) * up).astype(jnp.bfloat16)

    def apply_layer(rows, memory, totals):
        normed = gather_rows(rms_norm(rows, gain_one))
        both = jnp.einsum(
            "sd,hdc->shc", normed, qkv_pair, preferred_element_type=jnp.float32
        ).astype(jnp.bfloat16)
        swapped = swap_halves(both[:, ::-1, head_dim:])
        queries = both[..., :head_dim]
        keyed = jnp.concatenate([both[..., head_dim : 2 * head_dim], swapped[..., :head_dim]], axis=0)
        valued = jnp.concatenate([both[..., 2 * head_dim :], swapped[..., head_dim:]], axis=0)
        blended = attend(queries, keyed, valued, memory, totals, logits, allowed)
        memory, totals = absorb(keyed, valued, memory, totals)
        attn = jnp.dot(
            blended.reshape(half_len, -1), out_pair, preferred_element_type=jnp.float32
        )
        attn = scatter_sum(attn.astype(jnp.bfloat16))
        hidden_one = (rows.astype(jnp.float32) + attn).astype(jnp.bfloat16)
        normed_two = gather_rows(rms_norm(hidden_one, gain_two))
        down = jnp.dot(expand(normed_two), down_pair, preferred_element_type=jnp.float32)
        ffn = scatter_sum(down.astype(jnp.bfloat16))
        output = (hidden_one.astype(jnp.float32) + ffn).astype(jnp.bfloat16)
        return (output, memory, totals)

    first_rows, memory_one, totals_one = apply_layer(acts, memory_pair, totals_pair)
    incoming = next_layer(first_rows)
    fresh_rows = lax.dynamic_index_in_dim(fresh, half, 0, keepdims=False)
    entering = jnp.where(depth == 0, fresh_rows, incoming)
    second_rows, memory_two, totals_two = apply_layer(entering, memory_one, totals_one)
    return (first_rows, second_rows, memory_two[:1], totals_two[:1])


def solution(mesh):
    in_specs = (
        P(("layer", "tp"), None),
        P(None, "tp", None),
        P(),
        P(),
        P(("layer", "tp"), None, None),
        P(("layer", "tp"), None),
        P(None, None, ("layer", "tp")),
        P(("layer", "tp"), None),
        P(("layer", "tp"), None, None),
        P(("layer", "tp"), None),
        P(("layer", "tp")),
    )
    out_specs = (
        P(("layer", "tp"), None),
        P(("layer", "tp"), None),
        P(("layer", "tp"), None, None),
        P(("layer", "tp"), None),
    )
    return jax.shard_map(body, mesh=mesh, in_specs=in_specs, out_specs=out_specs, check_vma=False)
```

```python
import jax
import jax.numpy as jnp
from jax import lax
from jax.experimental import pallas as pl
from jax.experimental.pallas import tpu as pltpu
from jax.sharding import PartitionSpec as P


def swap_halves(value):
    pairs = [(source, source ^ 1) for source in range(lax.axis_size("layer"))]
    return lax.ppermute(value, "layer", pairs)


def next_layer(value):
    count = lax.axis_size("layer")
    return lax.ppermute(value, "layer", [(source, source + 2) for source in range(count - 2)])


def exchange(blocks):
    return lax.all_to_all(blocks, "tp", 0, 0, tiled=True)


def gather_rows(rows):
    members = lax.axis_size("tp")
    blocks = exchange(jnp.broadcast_to(rows[None], (members,) + rows.shape))
    return blocks.reshape((-1, rows.shape[1]))


def scatter_sum(partial, *beside):
    members = lax.axis_size("tp")
    blocks = exchange(partial.reshape((members, -1, partial.shape[1])))
    if beside:
        blocks, *beside = lax.optimization_barrier((blocks, *beside))
    return (jnp.sum(blocks.astype(jnp.float32), axis=0), *beside)


def feed_kernel(rows_ref, wide_ref, down_ref, out_ref, total_ref):
    step = pl.program_id(0)
    gate, up = (
        jnp.dot(rows_ref[...], wide_ref[0, part], preferred_element_type=jnp.float32)
        for part in range(2)
    )
    hidden = (jax.nn.silu(gate) * up).astype(jnp.bfloat16)
    term = jnp.dot(hidden, down_ref[0], preferred_element_type=jnp.float32)

    @pl.when(step == 0)
    def _():
        total_ref[...] = term

    @pl.when(step > 0)
    def _():
        total_ref[...] += term

    @pl.when(step == pl.num_programs(0) - 1)
    def _():
        out_ref[...] = total_ref[...].astype(out_ref.dtype)


def feed_forward(rows, wide_pair, down_pair, cut=2):
    count, width = rows.shape
    sources, _, _, units = wide_pair.shape
    block = units // cut
    return pl.pallas_call(
        feed_kernel,
        grid=(sources * cut,),
        out_shape=jax.ShapeDtypeStruct((count, width), rows.dtype),
        in_specs=[
            pl.BlockSpec((count, width), lambda i: (0, 0)),
            pl.BlockSpec((1, 2, width, block), lambda i: (i // cut, 0, 0, i % cut)),
            pl.BlockSpec((1, block, width), lambda i: (i // cut, i % cut, 0)),
        ],
        out_specs=pl.BlockSpec((count, width), lambda i: (0, 0)),
        scratch_shapes=[pltpu.VMEM((count, width), jnp.float32)],
        name="feed_forward",
    )(rows, wide_pair, down_pair)


def rms_norm(values, weight):
    floats = values.astype(jnp.float32)
    scaled = floats * lax.rsqrt(jnp.mean(floats * floats, axis=-1, keepdims=True) + 1e-05)
    return (scaled * weight).astype(jnp.bfloat16)


def lifted(values):
    return jax.nn.elu(values.astype(jnp.float32)) + 1.0


def attend(queries, keyed, valued, memory, totals, logits, allowed):
    head_dim = memory.shape[-1]
    scores = jnp.einsum(
        "qhc,khc->hqk", queries, keyed, preferred_element_type=jnp.float32
    ) * head_dim ** (-0.5)
    probs = jax.nn.softmax(jnp.where(allowed[None], scores, -jnp.inf), axis=-1).astype(jnp.bfloat16)
    direct = jnp.einsum("hqk,khc->qhc", probs, valued, preferred_element_type=jnp.float32)
    lifted_q = lifted(queries)
    numer = jnp.einsum("qhc,hce->qhe", lifted_q, memory, precision=lax.Precision.HIGHEST)
    denom = jnp.einsum("qhc,hc->qh", lifted_q, totals, precision=lax.Precision.HIGHEST)[..., None]
    gate_open = jax.nn.sigmoid(logits)[None, :, None]
    return (gate_open * numer / denom + (1.0 - gate_open) * direct).astype(jnp.bfloat16)


def absorb(keyed, valued, memory, totals):
    lifted_k = lifted(keyed)
    new_memory = memory + jnp.einsum(
        "khc,khe->hce", lifted_k, valued.astype(jnp.float32), precision=lax.Precision.HIGHEST
    )
    return (new_memory, totals + jnp.sum(lifted_k, axis=0))


def body(
    acts,
    fresh,
    norm_first,
    norm_second,
    proj_qkv,
    proj_out,
    proj_gate_up,
    proj_down,
    memory_state,
    memory_norm,
    bias_gate,
):
    position = lax.axis_index("layer")
    half = position % 2
    depth = position // 2
    gain_one = lax.dynamic_index_in_dim(norm_first, depth, 0, keepdims=False)
    gain_two = lax.dynamic_index_in_dim(norm_second, depth, 0, keepdims=False)
    head_dim = memory_state.shape[-1]
    half_len = acts.shape[0] * lax.axis_size("tp")
    logit_row = jnp.broadcast_to(bias_gate[:, None, None], (1, 1, head_dim))
    state = jnp.concatenate([memory_state, memory_norm[:, None], logit_row], axis=1)
    other_state = swap_halves(state)
    other_qkv = swap_halves(proj_qkv)
    out_pair = lax.optimization_barrier(
        jnp.concatenate([proj_out, swap_halves(proj_out)], axis=0)
    )
    wide = lax.optimization_barrier(jnp.transpose(proj_gate_up, (1, 0, 2)))
    wide_pair, down_pair = (
        lax.optimization_barrier(jnp.stack([weight, swap_halves(weight)], axis=0))
        for weight in (wide, proj_down)
    )
    fresh_rows = lax.dynamic_index_in_dim(fresh, half, 0, keepdims=False)
    memory_pair = jnp.concatenate([memory_state, other_state[:, :head_dim]], axis=0)
    totals_pair = jnp.concatenate([memory_norm, other_state[:, head_dim]], axis=0)
    logits = jnp.concatenate([bias_gate, other_state[:, head_dim + 1, 0]], axis=0)
    index = jnp.arange(half_len)
    causal = index[:, None] >= index[None, :]
    allowed = jnp.concatenate([causal, jnp.broadcast_to(half == 1, causal.shape)], axis=1)

    def project(rows, weight):
        return jnp.dot(rows, weight[0], preferred_element_type=jnp.float32).astype(jnp.bfloat16)

    def apply_layer(rows, memory, totals, *beside):
        normed = gather_rows(rms_norm(rows, gain_one))
        own = project(normed, proj_qkv)
        other = project(normed, other_qkv)
        swapped = swap_halves(jnp.stack([other[:, head_dim:], own[:, head_dim:]], axis=1))
        both = jnp.stack([own, other], axis=1)
        queries = both[..., :head_dim]
        keyed = jnp.concatenate([both[..., head_dim : 2 * head_dim], swapped[..., :head_dim]], axis=0)
        valued = jnp.concatenate([both[..., 2 * head_dim :], swapped[..., head_dim:]], axis=0)
        blended = attend(queries, keyed, valued, memory, totals, logits, allowed)
        memory, totals = absorb(keyed, valued, memory, totals)
        attn = jnp.dot(
            blended.reshape(half_len, -1), out_pair, preferred_element_type=jnp.float32
        )
        attn, memory, totals, *beside = scatter_sum(
            attn.astype(jnp.bfloat16), memory, totals, *beside
        )
        hidden_one = (rows.astype(jnp.float32) + attn).astype(jnp.bfloat16)
        normed_two = gather_rows(rms_norm(hidden_one, gain_two))
        (ffn,) = scatter_sum(feed_forward(normed_two, wide_pair, down_pair))
        output = (hidden_one.astype(jnp.float32) + ffn).astype(jnp.bfloat16)
        return (output, memory, totals, *beside)

    first_rows, memory_one, totals_one, fresh_rows = apply_layer(
        acts, memory_pair, totals_pair, fresh_rows
    )
    incoming = next_layer(first_rows)
    entering = jnp.where(depth == 0, fresh_rows, incoming)
    second_rows, memory_two, totals_two = apply_layer(entering, memory_one, totals_one)
    return (first_rows, second_rows, memory_two[:1], totals_two[:1])


def solution(mesh):
    in_specs = (
        P(("layer", "tp"), None),
        P(None, "tp", None),
        P(),
        P(),
        P(("layer", "tp"), None, None),
        P(("layer", "tp"), None),
        P(None, None, ("layer", "tp")),
        P(("layer", "tp"), None),
        P(("layer", "tp"), None, None),
        P(("layer", "tp"), None),
        P(("layer", "tp")),
    )
    out_specs = (
        P(("layer", "tp"), None),
        P(("layer", "tp"), None),
        P(("layer", "tp"), None, None),
        P(("layer", "tp"), None),
    )
    return jax.shard_map(body, mesh=mesh, in_specs=in_specs, out_specs=out_specs, check_vma=False)
```

```python
import jax
import jax.numpy as jnp
from jax import lax
from jax.sharding import PartitionSpec as P


def swap_halves(value):
    pairs = [(source, source ^ 1) for source in range(lax.axis_size("layer"))]
    return lax.ppermute(value, "layer", pairs)


def next_layer(value):
    count = lax.axis_size("layer")
    return lax.ppermute(value, "layer", [(source, source + 2) for source in range(count - 2)])


def exchange(blocks):
    return lax.all_to_all(blocks, "tp", 0, 0, tiled=True)


def gather_rows(rows):
    members = lax.axis_size("tp")
    blocks = exchange(jnp.broadcast_to(rows[None], (members,) + rows.shape))
    return blocks.reshape((-1, rows.shape[1]))


def scatter_sum(partial, *beside):
    members = lax.axis_size("tp")
    blocks = exchange(partial.reshape((members, -1, partial.shape[1])))
    if beside:
        blocks, *beside = lax.optimization_barrier((blocks, *beside))
    return (jnp.sum(blocks.astype(jnp.float32), axis=0), *beside)


def feed_forward(rows, wide, other_wide, down_pair):
    hidden = []
    for weight in (wide, other_wide):
        gate_up = jnp.einsum("sd,tdf->stf", rows, weight, preferred_element_type=jnp.float32)
        hidden.append((jax.nn.silu(gate_up[:, 0]) * gate_up[:, 1]).astype(jnp.bfloat16))
    hidden = jnp.concatenate(hidden, axis=1)
    return jnp.dot(hidden, down_pair, preferred_element_type=jnp.float32).astype(jnp.bfloat16)


def rms_norm(values, weight):
    floats = values.astype(jnp.float32)
    scaled = floats * lax.rsqrt(jnp.mean(floats * floats, axis=-1, keepdims=True) + 1e-05)
    return (scaled * weight).astype(jnp.bfloat16)


def lifted(values):
    return jax.nn.elu(values.astype(jnp.float32)) + 1.0


def attend(queries, keyed, valued, memory, totals, logits, allowed):
    head_dim = memory.shape[-1]
    scores = jnp.einsum(
        "qhc,khc->hqk", queries, keyed, preferred_element_type=jnp.float32
    ) * head_dim ** (-0.5)
    probs = jax.nn.softmax(jnp.where(allowed[None], scores, -jnp.inf), axis=-1).astype(jnp.bfloat16)
    direct = jnp.einsum("hqk,khc->qhc", probs, valued, preferred_element_type=jnp.float32)
    lifted_q = lifted(queries)
    numer = jnp.einsum("qhc,hce->qhe", lifted_q, memory, precision=lax.Precision.HIGHEST)
    denom = jnp.einsum("qhc,hc->qh", lifted_q, totals, precision=lax.Precision.HIGHEST)[..., None]
    gate_open = jax.nn.sigmoid(logits)[None, :, None]
    return (gate_open * numer / denom + (1.0 - gate_open) * direct).astype(jnp.bfloat16)


def absorb(keyed, valued, memory, totals):
    lifted_k = lifted(keyed)
    new_memory = memory + jnp.einsum(
        "khc,khe->hce", lifted_k, valued.astype(jnp.float32), precision=lax.Precision.HIGHEST
    )
    return (new_memory, totals + jnp.sum(lifted_k, axis=0))


def body(
    acts,
    fresh,
    norm_first,
    norm_second,
    proj_qkv,
    proj_out,
    proj_gate_up,
    proj_down,
    memory_state,
    memory_norm,
    bias_gate,
):
    position = lax.axis_index("layer")
    half = position % 2
    depth = position // 2
    gain_one = lax.dynamic_index_in_dim(norm_first, depth, 0, keepdims=False)
    gain_two = lax.dynamic_index_in_dim(norm_second, depth, 0, keepdims=False)
    head_dim = memory_state.shape[-1]
    half_len = acts.shape[0] * lax.axis_size("tp")
    logit_row = jnp.broadcast_to(bias_gate[:, None, None], (1, 1, head_dim))
    state = jnp.concatenate([memory_state, memory_norm[:, None], logit_row], axis=1)
    other_state = swap_halves(state)
    other_qkv = swap_halves(proj_qkv)
    out_pair = lax.optimization_barrier(
        jnp.concatenate([proj_out, swap_halves(proj_out)], axis=0)
    )
    wide = lax.optimization_barrier(jnp.transpose(proj_gate_up, (1, 0, 2)))
    other_wide = swap_halves(wide)
    down_pair = jnp.concatenate([proj_down, swap_halves(proj_down)], axis=0)
    feed_weights = lax.optimization_barrier((wide, other_wide, down_pair))
    fresh_rows = lax.dynamic_index_in_dim(fresh, half, 0, keepdims=False)
    memory_pair = jnp.concatenate([memory_state, other_state[:, :head_dim]], axis=0)
    totals_pair = jnp.concatenate([memory_norm, other_state[:, head_dim]], axis=0)
    logits = jnp.concatenate([bias_gate, other_state[:, head_dim + 1, 0]], axis=0)
    index = jnp.arange(half_len)
    causal = index[:, None] >= index[None, :]
    allowed = jnp.concatenate([causal, jnp.broadcast_to(half == 1, causal.shape)], axis=1)

    def project(rows, weight):
        return jnp.dot(rows, weight[0], preferred_element_type=jnp.float32).astype(jnp.bfloat16)

    def apply_layer(rows, memory, totals, wide, other_wide, down_pair, *beside):
        normed = gather_rows(rms_norm(rows, gain_one))
        own = project(normed, proj_qkv)
        other = project(normed, other_qkv)
        swapped = swap_halves(jnp.stack([other[:, head_dim:], own[:, head_dim:]], axis=1))
        both = jnp.stack([own, other], axis=1)
        queries = both[..., :head_dim]
        keyed = jnp.concatenate([both[..., head_dim : 2 * head_dim], swapped[..., :head_dim]], axis=0)
        valued = jnp.concatenate([both[..., 2 * head_dim :], swapped[..., head_dim:]], axis=0)
        blended = attend(queries, keyed, valued, memory, totals, logits, allowed)
        memory, totals = absorb(keyed, valued, memory, totals)
        attn = jnp.dot(
            blended.reshape(half_len, -1), out_pair, preferred_element_type=jnp.float32
        )
        attn, memory, totals, wide, other_wide, down_pair, *beside = scatter_sum(
            attn.astype(jnp.bfloat16), memory, totals, wide, other_wide, down_pair, *beside
        )
        hidden_one = (rows.astype(jnp.float32) + attn).astype(jnp.bfloat16)
        normed_two = gather_rows(rms_norm(hidden_one, gain_two))
        (ffn,) = scatter_sum(feed_forward(normed_two, wide, other_wide, down_pair))
        output = (hidden_one.astype(jnp.float32) + ffn).astype(jnp.bfloat16)
        return (output, memory, totals, wide, other_wide, down_pair, *beside)

    first_rows, memory_one, totals_one, *feed_weights, fresh_rows = apply_layer(
        acts, memory_pair, totals_pair, *feed_weights, fresh_rows
    )
    incoming = next_layer(first_rows)
    entering = jnp.where(depth == 0, fresh_rows, incoming)
    second_rows, memory_two, totals_two, *_ = apply_layer(
        entering, memory_one, totals_one, *feed_weights
    )
    return (first_rows, second_rows, memory_two[:1], totals_two[:1])


def solution(mesh):
    in_specs = (
        P(("layer", "tp"), None),
        P(None, "tp", None),
        P(),
        P(),
        P(("layer", "tp"), None, None),
        P(("layer", "tp"), None),
        P(None, None, ("layer", "tp")),
        P(("layer", "tp"), None),
        P(("layer", "tp"), None, None),
        P(("layer", "tp"), None),
        P(("layer", "tp")),
    )
    out_specs = (
        P(("layer", "tp"), None),
        P(("layer", "tp"), None),
        P(("layer", "tp"), None, None),
        P(("layer", "tp"), None),
    )
    return jax.shard_map(body, mesh=mesh, in_specs=in_specs, out_specs=out_specs, check_vma=False)
```

```python
import jax
import jax.numpy as jnp
from jax import lax
from jax.experimental import pallas as pl
from jax.experimental.pallas import tpu as pltpu
from jax.sharding import PartitionSpec as P


def swap_halves(value):
    pairs = [(source, source ^ 1) for source in range(lax.axis_size("layer"))]
    return lax.ppermute(value, "layer", pairs)


def next_layer(value):
    count = lax.axis_size("layer")
    return lax.ppermute(value, "layer", [(source, source + 2) for source in range(count - 2)])


def exchange(blocks):
    return lax.all_to_all(blocks, "tp", 0, 0, tiled=True)


def spread(rows):
    return jnp.broadcast_to(rows[None], (lax.axis_size("tp"),) + rows.shape)


def gather_rows(blocks):
    return exchange(blocks).reshape((-1, blocks.shape[2]))


def scatter_sum(partial, *beside):
    members = lax.axis_size("tp")
    blocks = exchange(partial.reshape((members, -1, partial.shape[1])))
    if beside:
        blocks, *beside = lax.optimization_barrier((blocks, *beside))
    return (jnp.sum(blocks.astype(jnp.float32), axis=0), *beside)


def feed_forward(rows, wide, other_wide, down, other_down):
    total = None
    for weight, narrow in ((wide, down), (other_wide, other_down)):
        gate_up = jnp.einsum("sd,dtf->stf", rows, weight, preferred_element_type=jnp.float32)
        hidden = (jax.nn.silu(gate_up[:, 0]) * gate_up[:, 1]).astype(jnp.bfloat16)
        term = jnp.dot(hidden, narrow, preferred_element_type=jnp.float32)
        total = term if total is None else total + term
    return total.astype(jnp.bfloat16)


def rms_norm(values, weight):
    floats = values.astype(jnp.float32)
    scaled = floats * lax.rsqrt(jnp.mean(floats * floats, axis=-1, keepdims=True) + 1e-05)
    return (scaled * weight).astype(jnp.bfloat16)


def first_kernel(rows_ref, gains_ref, out_ref):
    depth = lax.axis_index("layer") // 2
    normed = rms_norm(rows_ref[...], gains_ref[pl.ds(depth, 1), :])
    for member in range(out_ref.shape[0]):
        out_ref[member] = normed


def first_blocks(rows, gains):
    members = lax.axis_size("tp")
    return pl.pallas_call(
        first_kernel,
        out_shape=jax.ShapeDtypeStruct((members,) + rows.shape, rows.dtype),
        in_specs=[pl.BlockSpec(memory_space=pltpu.VMEM)] * 2,
        out_specs=pl.BlockSpec(memory_space=pltpu.VMEM),
        name="first_blocks",
    )(rows, gains)


def lifted(values):
    return jax.nn.elu(values.astype(jnp.float32)) + 1.0


def attend(queries, keyed, valued, memory, totals, logits, allowed):
    head_dim = memory.shape[-1]
    scores = jnp.einsum(
        "qhc,khc->hqk", queries, keyed, preferred_element_type=jnp.float32
    ) * head_dim ** (-0.5)
    probs = jax.nn.softmax(jnp.where(allowed[None], scores, -jnp.inf), axis=-1).astype(jnp.bfloat16)
    direct = jnp.einsum("hqk,khc->qhc", probs, valued, preferred_element_type=jnp.float32)
    lifted_q = lifted(queries)
    numer = jnp.einsum("qhc,hce->qhe", lifted_q, memory, precision=lax.Precision.HIGHEST)
    denom = jnp.einsum("qhc,hc->qh", lifted_q, totals, precision=lax.Precision.HIGHEST)[..., None]
    gate_open = jax.nn.sigmoid(logits)[None, :, None]
    return (gate_open * numer / denom + (1.0 - gate_open) * direct).astype(jnp.bfloat16)


def absorb(keyed, valued, memory, totals):
    lifted_k = lifted(keyed)
    new_memory = memory + jnp.einsum(
        "khc,khe->hce", lifted_k, valued.astype(jnp.float32), precision=lax.Precision.HIGHEST
    )
    return (new_memory, totals + jnp.sum(lifted_k, axis=0))


def body(
    acts,
    fresh,
    norm_first,
    norm_second,
    proj_qkv,
    proj_out,
    proj_gate_up,
    proj_down,
    memory_state,
    memory_norm,
    bias_gate,
):
    position = lax.axis_index("layer")
    half = position % 2
    depth = position // 2
    gain_one = lax.dynamic_index_in_dim(norm_first, depth, 0, keepdims=False)
    gain_two = lax.dynamic_index_in_dim(norm_second, depth, 0, keepdims=False)
    head_dim = memory_state.shape[-1]
    half_len = acts.shape[0] * lax.axis_size("tp")
    logit_row = jnp.broadcast_to(bias_gate[:, None, None], (1, 1, head_dim))
    state = jnp.concatenate([memory_state, memory_norm[:, None], logit_row], axis=1)
    other_state = swap_halves(state)
    other_qkv = swap_halves(proj_qkv)
    out_pair = lax.optimization_barrier(
        jnp.concatenate([proj_out, swap_halves(proj_out)], axis=0)
    )
    other_wide = swap_halves(proj_gate_up)
    other_down = swap_halves(proj_down)
    fresh_rows = lax.dynamic_index_in_dim(fresh, half, 0, keepdims=False)
    memory_pair = jnp.concatenate([memory_state, other_state[:, :head_dim]], axis=0)
    totals_pair = jnp.concatenate([memory_norm, other_state[:, head_dim]], axis=0)
    logits = jnp.concatenate([bias_gate, other_state[:, head_dim + 1, 0]], axis=0)
    index = jnp.arange(half_len)
    causal = index[:, None] >= index[None, :]
    allowed = jnp.concatenate([causal, jnp.broadcast_to(half == 1, causal.shape)], axis=1)

    def project(rows, weight):
        return jnp.dot(rows, weight[0], preferred_element_type=jnp.float32).astype(jnp.bfloat16)

    def apply_layer(rows, blocks, memory, totals, other_wide, other_down, *beside):
        normed = gather_rows(blocks)
        own = project(normed, proj_qkv)
        other = project(normed, other_qkv)
        swapped = swap_halves(jnp.stack([other[:, head_dim:], own[:, head_dim:]], axis=1))
        both = jnp.stack([own, other], axis=1)
        queries = both[..., :head_dim]
        keyed = jnp.concatenate([both[..., head_dim : 2 * head_dim], swapped[..., :head_dim]], axis=0)
        valued = jnp.concatenate([both[..., 2 * head_dim :], swapped[..., head_dim:]], axis=0)
        blended = attend(queries, keyed, valued, memory, totals, logits, allowed)
        memory, totals = absorb(keyed, valued, memory, totals)
        attn = jnp.dot(
            blended.reshape(half_len, -1), out_pair, preferred_element_type=jnp.float32
        )
        attn, memory, totals, other_down, *beside = scatter_sum(
            attn.astype(jnp.bfloat16), memory, totals, other_down, *beside
        )
        hidden_one = (rows.astype(jnp.float32) + attn).astype(jnp.bfloat16)
        normed_two = gather_rows(spread(rms_norm(hidden_one, gain_two)))
        (ffn,) = scatter_sum(
            feed_forward(normed_two, proj_gate_up, other_wide, proj_down, other_down)
        )
        output = (hidden_one.astype(jnp.float32) + ffn).astype(jnp.bfloat16)
        return (output, memory, totals, other_wide, other_down, *beside)

    first_rows, memory_one, totals_one, other_wide, other_down, fresh_rows = apply_layer(
        acts, first_blocks(acts, norm_first), memory_pair, totals_pair, other_wide, other_down, fresh_rows
    )
    incoming = next_layer(first_rows)
    entering = jnp.where(depth == 0, fresh_rows, incoming)
    second_rows, memory_two, totals_two, *_ = apply_layer(
        entering, spread(rms_norm(entering, gain_one)), memory_one, totals_one, other_wide, other_down
    )
    return (first_rows, second_rows, memory_two[:1], totals_two[:1])


def solution(mesh):
    in_specs = (
        P(("layer", "tp"), None),
        P(None, "tp", None),
        P(),
        P(),
        P(("layer", "tp"), None, None),
        P(("layer", "tp"), None),
        P(None, None, ("layer", "tp")),
        P(("layer", "tp"), None),
        P(("layer", "tp"), None, None),
        P(("layer", "tp"), None),
        P(("layer", "tp")),
    )
    out_specs = (
        P(("layer", "tp"), None),
        P(("layer", "tp"), None),
        P(("layer", "tp"), None, None),
        P(("layer", "tp"), None),
    )
    return jax.shard_map(body, mesh=mesh, in_specs=in_specs, out_specs=out_specs, check_vma=False)
```

```python
import jax
import jax.numpy as jnp
from jax import lax
from jax.experimental import pallas as pl
from jax.experimental.pallas import tpu as pltpu
from jax.sharding import PartitionSpec as P


def swap_halves(value):
    pairs = [(source, source ^ 1) for source in range(lax.axis_size("layer"))]
    return lax.ppermute(value, "layer", pairs)


def next_layer(value):
    count = lax.axis_size("layer")
    return lax.ppermute(value, "layer", [(source, source + 2) for source in range(count - 2)])


def exchange(blocks):
    return lax.all_to_all(blocks, "tp", 0, 0, tiled=True)


def spread(rows):
    return jnp.broadcast_to(rows[None], (lax.axis_size("tp"),) + rows.shape)


def gather_rows(blocks):
    return exchange(blocks).reshape((-1, blocks.shape[2]))


def scatter_sum(partial):
    members = lax.axis_size("tp")
    blocks = exchange(partial.reshape((members, -1, partial.shape[1])))
    return jnp.sum(blocks.astype(jnp.float32), axis=0)


def rms_norm(values, weight):
    floats = values.astype(jnp.float32)
    scaled = floats * lax.rsqrt(jnp.mean(floats * floats, axis=-1, keepdims=True) + 1e-05)
    return (scaled * weight).astype(jnp.bfloat16)


def first_kernel(rows_ref, gains_ref, out_ref):
    depth = lax.axis_index("layer") // 2
    normed = rms_norm(rows_ref[...], gains_ref[pl.ds(depth, 1), :])
    for member in range(out_ref.shape[0]):
        out_ref[member] = normed


def first_blocks(rows, gains):
    members = lax.axis_size("tp")
    return pl.pallas_call(
        first_kernel,
        out_shape=jax.ShapeDtypeStruct((members,) + rows.shape, rows.dtype),
        in_specs=[pl.BlockSpec(memory_space=pltpu.VMEM)] * 2,
        out_specs=pl.BlockSpec(memory_space=pltpu.VMEM),
        name="first_blocks",
    )(rows, gains)


def lifted(values):
    return jax.nn.elu(values.astype(jnp.float32)) + 1.0


def attend(queries, keyed, valued, memory, totals, logits, allowed):
    head_dim = memory.shape[-1]
    scores = jnp.einsum(
        "qhc,khc->hqk", queries, keyed, preferred_element_type=jnp.float32
    ) * head_dim ** (-0.5)
    probs = jax.nn.softmax(jnp.where(allowed[None], scores, -jnp.inf), axis=-1).astype(jnp.bfloat16)
    direct = jnp.einsum("hqk,khc->qhc", probs, valued, preferred_element_type=jnp.float32)
    lifted_q = lifted(queries)
    numer = jnp.einsum("qhc,hce->qhe", lifted_q, memory, precision=lax.Precision.HIGHEST)
    denom = jnp.einsum("qhc,hc->qh", lifted_q, totals, precision=lax.Precision.HIGHEST)[..., None]
    gate_open = jax.nn.sigmoid(logits)[None, :, None]
    return (gate_open * numer / denom + (1.0 - gate_open) * direct).astype(jnp.bfloat16)


def absorb(keyed, valued, memory, totals):
    lifted_k = lifted(keyed)
    new_memory = memory + jnp.einsum(
        "khc,khe->hce", lifted_k, valued.astype(jnp.float32), precision=lax.Precision.HIGHEST
    )
    return (new_memory, totals + jnp.sum(lifted_k, axis=0))


def body(
    acts,
    fresh,
    norm_first,
    norm_second,
    proj_qkv,
    proj_out,
    proj_gate_up,
    proj_down,
    memory_state,
    memory_norm,
    bias_gate,
):
    position = lax.axis_index("layer")
    half = position % 2
    depth = position // 2
    gain_one = lax.dynamic_index_in_dim(norm_first, depth, 0, keepdims=False)
    gain_two = lax.dynamic_index_in_dim(norm_second, depth, 0, keepdims=False)
    head_dim = memory_state.shape[-1]
    half_len = acts.shape[0] * lax.axis_size("tp")
    logit_row = jnp.broadcast_to(bias_gate[:, None, None], (1, 1, head_dim))
    state = jnp.concatenate([memory_state, memory_norm[:, None], logit_row], axis=1)
    other_state = swap_halves(state)
    wide = lax.optimization_barrier(jnp.transpose(proj_gate_up, (1, 0, 2)))
    other_qkv = swap_halves(proj_qkv)
    out_pair, wide_pair, down_pair = (
        lax.optimization_barrier(jnp.concatenate([weight, swap_halves(weight)], axis=axis))
        for weight, axis in ((proj_out, 0), (wide, 2), (proj_down, 0))
    )
    memory_pair = jnp.concatenate([memory_state, other_state[:, :head_dim]], axis=0)
    totals_pair = jnp.concatenate([memory_norm, other_state[:, head_dim]], axis=0)
    logits = jnp.concatenate([bias_gate, other_state[:, head_dim + 1, 0]], axis=0)
    index = jnp.arange(half_len)
    causal = index[:, None] >= index[None, :]
    allowed = jnp.concatenate([causal, jnp.broadcast_to(half == 1, causal.shape)], axis=1)

    def project(rows, weight):
        return jnp.dot(rows, weight[0], preferred_element_type=jnp.float32).astype(jnp.bfloat16)

    def expand(rows):
        gate, up = (
            jnp.dot(rows, weight, preferred_element_type=jnp.float32) for weight in wide_pair
        )
        return (jax.nn.silu(gate) * up).astype(jnp.bfloat16)

    def apply_layer(rows, blocks, memory, totals):
        normed = gather_rows(blocks)
        own = project(normed, proj_qkv)
        other = project(normed, other_qkv)
        swapped = swap_halves(jnp.stack([other[:, head_dim:], own[:, head_dim:]], axis=1))
        both = jnp.stack([own, other], axis=1)
        queries = both[..., :head_dim]
        keyed = jnp.concatenate([both[..., head_dim : 2 * head_dim], swapped[..., :head_dim]], axis=0)
        valued = jnp.concatenate([both[..., 2 * head_dim :], swapped[..., head_dim:]], axis=0)
        blended = attend(queries, keyed, valued, memory, totals, logits, allowed)
        memory, totals = absorb(keyed, valued, memory, totals)
        attn = jnp.dot(
            blended.reshape(half_len, -1), out_pair, preferred_element_type=jnp.float32
        )
        attn = scatter_sum(attn.astype(jnp.bfloat16))
        hidden_one = (rows.astype(jnp.float32) + attn).astype(jnp.bfloat16)
        normed_two = gather_rows(spread(rms_norm(hidden_one, gain_two)))
        down = jnp.dot(expand(normed_two), down_pair, preferred_element_type=jnp.float32)
        ffn = scatter_sum(down.astype(jnp.bfloat16))
        output = (hidden_one.astype(jnp.float32) + ffn).astype(jnp.bfloat16)
        return (output, memory, totals)

    first_rows, memory_one, totals_one = apply_layer(acts, first_blocks(acts, norm_first), memory_pair, totals_pair)
    incoming = next_layer(first_rows)
    fresh_rows = lax.dynamic_index_in_dim(fresh, half, 0, keepdims=False)
    entering = jnp.where(depth == 0, fresh_rows, incoming)
    second_rows, memory_two, totals_two = apply_layer(entering, spread(rms_norm(entering, gain_one)), memory_one, totals_one)
    return (first_rows, second_rows, memory_two[:1], totals_two[:1])


def solution(mesh):
    in_specs = (
        P(("layer", "tp"), None),
        P(None, "tp", None),
        P(),
        P(),
        P(("layer", "tp"), None, None),
        P(("layer", "tp"), None),
        P(None, None, ("layer", "tp")),
        P(("layer", "tp"), None),
        P(("layer", "tp"), None, None),
        P(("layer", "tp"), None),
        P(("layer", "tp")),
    )
    out_specs = (
        P(("layer", "tp"), None),
        P(("layer", "tp"), None),
        P(("layer", "tp"), None, None),
        P(("layer", "tp"), None),
    )
    return jax.shard_map(body, mesh=mesh, in_specs=in_specs, out_specs=out_specs, check_vma=False)
```
